32 devices in a mesh: groups: 2 (over y), seq: 16 (over z, x, core).
Axes of the slice: x: 2, y: 2, z: 4, core: 2. Of those that a mesh axis runs over, the one named last changes fastest.
Arguments:
- queries: bfloat16 [8192, 2048], P(('groups', 'seq')), parts along dimension 0, may hold values from -6 to 6
- keys: bfloat16 [8192, 1024], P(('groups', 'seq')), parts along dimension 0, may hold values from -6 to 6
- values: bfloat16 [8192, 1024], P(('groups', 'seq')), parts along dimension 0, may hold values from -6 to 6
- out_grad: bfloat16 [8192, 2048], P(('groups', 'seq')), parts along dimension 0, may hold values from -6 to 6
Outputs:
- attended: bfloat16 [8192, 2048], P(('groups', 'seq')), parts along dimension 0
- query_grad: bfloat16 [8192, 2048], P(('groups', 'seq')), parts along dimension 0
- key_grad: bfloat16 [8192, 1024], P(('groups', 'seq')), parts along dimension 0
- value_grad: bfloat16 [8192, 1024], P(('groups', 'seq')), parts along dimension 0
The draws below stay inside these ranges and needn't reach their ends.
There are 2 independent parts, one for each index of `groups`. The reference program is written for one: setup_inputs(seed, part) draws one part's arguments, and reference() takes and returns one part's arrays. A program takes and returns all parts, laid end to end along the dimension named above; each array names one. Nothing has to cross between parts.
All inputs are finite; a program needn't handle non-finite values.
Results may differ from the reference program's by a relative error of at most 0.013.
Values may be sent and summed in bfloat16 or wider, within the bound.
A program may use at most 64 MiB of HBM per device.

```python
import jax
import jax.numpy as jnp
from jax import lax

HQ = 16
HK = 8
HD = 128
WINDOW = 1024
TOK_DEV = 256
TOKENS = 4096


def draw_queries(key, part):
    result = jnp.clip(jax.random.normal(jax.random.fold_in(key, 1), (TOKENS, HQ * HD), jnp.float32), -4.0, 4.0)
    return result.astype(jnp.bfloat16)


def draw_keys(key, part):
    result = jnp.clip(jax.random.normal(jax.random.fold_in(key, 2), (TOKENS, HK * HD), jnp.float32), -4.0, 4.0)
    return result.astype(jnp.bfloat16)


def level_of(own_key, shape, shards, smallest, high):
    def one(position, blocks):
        draws = jax.random.uniform(jax.random.fold_in(jax.random.fold_in(own_key, 6), position), (blocks,), jnp.float32, smallest / len(shards), high / len(shards))
        return jnp.repeat(jnp.exp(draws), shape[position] // blocks).reshape((-1,) + (1,) * (len(shape) - position - 1))

    gain = one(*shards[0])
    for cut in shards[1:]:
        gain = gain * one(*cut)
    return gain


def normal_values(own_key, shape, spread, bound, cuts=(), kind=jnp.bfloat16):
    factor_of = level_of(own_key, shape, cuts, -0.22, 0.18) if cuts else 1.0
    values = jax.random.normal(own_key, shape, jnp.float32) * spread * factor_of
    return jnp.minimum(jnp.maximum(values, -bound), bound).astype(kind)


def setup_inputs(seed: int = 0, part: int = 0) -> dict:
    key_of = jax.random.split(jax.random.key(seed), 5)
    part_keys = jax.random.split(jax.random.fold_in(key_of[4], part), 5)
    queries = draw_queries(jax.random.fold_in(jax.random.fold_in(key_of[4], part), 71), part)
    keys = draw_keys(jax.random.fold_in(jax.random.fold_in(key_of[4], part), 71), part)
    values = normal_values(part_keys[2], (TOKENS, HK * HD), 1.0, 6.0, ((0, 16),))
    out_grad = normal_values(part_keys[3], (TOKENS, HQ * HD), 1.0, 6.0, ((0, 16),))
    return dict(queries=queries, keys=keys, values=values, out_grad=out_grad)


query_scale = 168.0 ** -0.5


def head_block(query_head, key_head, value_head, grad_head, first):
    rows = query_head.shape[0]
    extent = key_head.shape[0]
    row_ids = jnp.arange(rows, dtype=jnp.int32)[:, None]
    col_ids = jnp.arange(extent, dtype=jnp.int32)[None, :]
    keep = (col_ids > row_ids) & (col_ids <= row_ids + (extent - rows)) & (first + col_ids >= 0)
    query_f = query_head.astype(jnp.float32)
    key_f = key_head.astype(jnp.float32)
    value_f = value_head.astype(jnp.float32)
    grad_f = grad_head.astype(jnp.float32)
    scores = jnp.einsum('rgd,kd->grk', query_f, key_f) * query_scale
    scores = jnp.where(keep[None], scores, jnp.float32(-1e30))
    peak = jnp.max(scores, axis=-1, keepdims=True)
    expo = jnp.exp(scores - peak)
    prob = expo / jnp.sum(expo, axis=-1, keepdims=True)
    prob_b = prob.astype(jnp.bfloat16)
    prob_bf = prob_b.astype(jnp.float32)
    attended = jnp.einsum('grk,kd->rgd', prob_bf, value_f).astype(jnp.bfloat16)
    dprob = jnp.einsum('rgd,kd->grk', grad_f, value_f)
    delta = jnp.sum(prob_bf * dprob, axis=-1, keepdims=True)
    dscore = (query_scale * prob * (dprob - delta)).astype(jnp.bfloat16)
    dscore_f = dscore.astype(jnp.float32)
    query_grad = jnp.einsum('grk,kd->rgd', dscore_f, key_f).astype(jnp.bfloat16)
    key_grad = jnp.einsum('grk,rgd->kd', dscore_f, query_f)
    value_grad = jnp.einsum('grk,rgd->kd', prob_bf, grad_f)
    return attended, query_grad, key_grad, value_grad


def attend(query_rows, key_rows, value_rows, grad_rows, first):
    rows = query_rows.shape[0]
    extent = key_rows.shape[0]
    group = HQ // HK
    query_heads = query_rows.reshape(rows, HK, group, HD).transpose(1, 0, 2, 3)
    grad_heads = grad_rows.reshape(rows, HK, group, HD).transpose(1, 0, 2, 3)
    key_heads = key_rows.reshape(extent, HK, HD).transpose(1, 0, 2)
    value_heads = value_rows.reshape(extent, HK, HD).transpose(1, 0, 2)

    def one_head(pieces):
        return head_block(pieces[0], pieces[1], pieces[2], pieces[3], first)

    attended, query_grad, key_grad, value_grad = lax.map(one_head, (query_heads, key_heads, value_heads, grad_heads))
    attended = attended.transpose(1, 0, 2, 3).reshape(rows, HQ * HD)
    query_grad = query_grad.transpose(1, 0, 2, 3).reshape(rows, HQ * HD)
    key_grad = key_grad.transpose(1, 0, 2).reshape(extent, HK * HD)
    value_grad = value_grad.transpose(1, 0, 2).reshape(extent, HK * HD)
    return attended, query_grad, key_grad, value_grad


def reference(queries, keys, values, out_grad):
    rows = TOK_DEV
    blocks = TOKENS // rows
    front = jnp.zeros((WINDOW, HK * HD), jnp.bfloat16)
    key_pad = jnp.concatenate([front, keys], axis=0)
    value_pad = jnp.concatenate([front, values], axis=0)
    key_acc = jnp.zeros((TOKENS + WINDOW, HK * HD), jnp.float32)
    value_acc = jnp.zeros((TOKENS + WINDOW, HK * HD), jnp.float32)

    def step(carry, block):
        key_sum, value_sum = carry
        start = (block * rows).astype(jnp.int32)
        query_rows = lax.dynamic_slice_in_dim(queries, start, rows, 0)
        grad_rows = lax.dynamic_slice_in_dim(out_grad, start, rows, 0)
        key_rows = lax.dynamic_slice_in_dim(key_pad, start, rows + WINDOW, 0)
        value_rows = lax.dynamic_slice_in_dim(value_pad, start, rows + WINDOW, 0)
        attended, query_grad, key_grad, value_grad = attend(query_rows, key_rows, value_rows, grad_rows, start - WINDOW)
        old_key = lax.dynamic_slice_in_dim(key_sum, start, rows + WINDOW, 0)
        old_value = lax.dynamic_slice_in_dim(value_sum, start, rows + WINDOW, 0)
        key_sum = lax.dynamic_update_slice_in_dim(key_sum, old_key + key_grad, start, 0)
        value_sum = lax.dynamic_update_slice_in_dim(value_sum, old_value + value_grad, start, 0)
        return (key_sum, value_sum), (attended, query_grad)

    (key_acc, value_acc), (attended, query_grad) = lax.scan(step, (key_acc, value_acc), jnp.arange(blocks, dtype=jnp.int32))
    attended = attended.reshape(TOKENS, HQ * HD)
    query_grad = query_grad.reshape(TOKENS, HQ * HD)
    key_grad = key_acc[WINDOW:].astype(jnp.bfloat16)
    value_grad = value_acc[WINDOW:].astype(jnp.bfloat16)
    return (attended, query_grad, key_grad, value_grad)
```

```python
import functools

import jax
import jax.numpy as jnp
from jax import lax
from jax.experimental import pallas as pl
from jax.experimental.pallas import tpu as pltpu
from jax.sharding import PartitionSpec as P

HQ = 16
HK = 8
HD = 128
WINDOW = 1024
REACH = 4
AHEAD = 3

query_scale = 168.0 ** (-0.5)


def product(left, right, left_dim, right_dim):
    return lax.dot_general(
        left, right, (((left_dim,), (right_dim,)), ((), ())), preferred_element_type=jnp.float32
    )


def kernel(
    quads,
    q_ref,
    g_ref,
    k_hbm,
    v_hbm,
    att_ref,
    dq_ref,
    dk_ref,
    dv_ref,
    kv,
    gacc,
    gm_out,
    gm_in,
    gx_out,
    gx_in,
    gz_out,
    gz_in,
    own_sem,
    z_send,
    z_recv,
    x_send,
    x_recv,
    m_send,
    m_recv,
    gz_send,
    gz_recv,
    gx_send,
    gx_recv,
    gm_send,
    gm_recv,
):
    rows = q_ref.shape[0]
    me = lax.axis_index("seq")
    quad = me // 4
    x = (me // 2) % 2
    core = me % 2
    other = me + 2 - 4 * x
    mate = me + 1 - 2 * core
    has_before = quad > 0
    has_after = quad < quads - 1
    after = jnp.where(has_after, me + 4, me)
    before = jnp.where(has_before, me - 4, me)

    def remote(src, dst, send, recv, target):
        return pltpu.make_async_remote_copy(
            src_ref=src,
            dst_ref=dst,
            send_sem=send,
            recv_sem=recv,
            device_id={"seq": target},
            device_id_type=pl.DeviceIdType.MESH,
        )

    def own_copy(h, which):
        source = (k_hbm, v_hbm)[which]
        return pltpu.make_async_copy(
            source.at[:, pl.ds(pl.multiple_of(h * HD, HD), HD)],
            kv.at[0, h, which],
            own_sem.at[which, h],
        )

    def to_after(h):
        return remote(kv.at[0, h], kv.at[4, h], z_send.at[h], z_recv.at[h], after)

    def to_other(h):
        return remote(kv.at[4 * x, h], kv.at[2, h], x_send.at[h], x_recv.at[h], other)

    def to_mate_a(h):
        return remote(
            kv.at[2, h], kv.at[3 - 2 * core, h], m_send.at[0, h], m_recv.at[0, h], mate
        )

    def to_mate_b(h):
        return remote(
            kv.at[4 * core, h], kv.at[1 + 2 * core, h], m_send.at[1, h], m_recv.at[1, h], mate
        )

    def grad_mate(h, which):
        return remote(
            gm_out.at[which, h],
            gm_in.at[which, h],
            gm_send.at[which, h],
            gm_recv.at[which, h],
            mate,
        )

    def grad_other(h):
        return remote(gx_out.at[h], gx_in.at[h], gx_send.at[h], gx_recv.at[h], other)

    def grad_before(h):
        return remote(gz_out.at[h], gz_in.at[h], gz_send.at[h], gz_recv.at[h], before)

    for h in range(HK):
        own_copy(h, 0).start()
        own_copy(h, 1).start()

    barrier = pltpu.get_barrier_semaphore()
    for target in (other, mate):
        pl.semaphore_signal(
            barrier, inc=1, device_id={"seq": target}, device_id_type=pl.DeviceIdType.MESH
        )

    @pl.when(has_before)
    def _():
        pl.semaphore_signal(
            barrier, inc=1, device_id={"seq": before}, device_id_type=pl.DeviceIdType.MESH
        )

    @pl.when(has_after)
    def _():
        pl.semaphore_signal(
            barrier, inc=1, device_id={"seq": after}, device_id_type=pl.DeviceIdType.MESH
        )

    @pl.when(jnp.logical_not(has_before))
    def _():
        kv[4] = jnp.zeros(kv.shape[1:], kv.dtype)

    pl.semaphore_wait(
        barrier, 2 + jnp.where(has_before, 1, 0) + jnp.where(has_after, 1, 0)
    )

    def start_after(h, carry):
        own_copy(h, 0).wait()
        own_copy(h, 1).wait()

        @pl.when(has_after)
        def _():
            to_after(h).start()

        return carry

    lax.fori_loop(0, HK, start_after, 0)

    def stage_other(h):
        @pl.when(has_before)
        def _():
            to_after(h).wait_recv()

        to_other(h).start()

    def stage_mate(h):
        to_other(h).wait_recv()
        to_mate_a(h).start()
        to_mate_b(h).start()

    key_ids = lax.broadcasted_iota(jnp.int32, (rows, rows), 0)
    query_ids = lax.broadcasted_iota(jnp.int32, (rows, rows), 1)

    def attend(h):
        extent = (REACH + 1) * rows
        key_all = kv[:, h, 0].reshape(extent, HD)
        value_all = kv[:, h, 1].reshape(extent, HD)
        key_grad = None
        value_grad = None
        for j in range(HQ // HK):
            columns = pl.ds(pl.multiple_of(h * (HQ // HK * HD) + j * HD, HD), HD)
            query = q_ref[:, columns]
            grad = g_ref[:, columns]
            scores = product(key_all, query, 1, 1) * query_scale
            parts = [scores[d * rows : (d + 1) * rows] for d in range(REACH + 1)]
            parts[0] = jnp.where(key_ids <= query_ids, parts[0], jnp.float32(-1e30))
            parts[REACH] = jnp.where(key_ids > query_ids, parts[REACH], jnp.float32(-1e30))
            outside = [
                jnp.where(me >= d, jnp.float32(0), jnp.float32(1e30)) for d in range(REACH + 1)
            ]
            peak = jnp.max(parts[0], axis=0, keepdims=True)
            for d in range(1, REACH + 1):
                peak = jnp.maximum(
                    peak, jnp.max(parts[d], axis=0, keepdims=True) - outside[d]
                )
            expo = jnp.concatenate(
                [jnp.exp(parts[d] - (peak + outside[d])) for d in range(REACH + 1)], axis=0
            )
            prob = expo * (1.0 / jnp.sum(expo, axis=0, keepdims=True))
            prob_b = prob.astype(jnp.bfloat16)
            attended = product(value_all, prob_b, 0, 0)
            att_ref[:, columns] = attended.T.astype(jnp.bfloat16)
            delta = jnp.sum(attended * grad.astype(jnp.float32).T, axis=0, keepdims=True)
            dprob = product(value_all, grad, 1, 1)
            dscore = (query_scale * prob * (dprob - delta)).astype(jnp.bfloat16)
            query_grad = product(key_all, dscore, 0, 0)
            dq_ref[:, columns] = query_grad.T.astype(jnp.bfloat16)
            key_part = product(dscore, query, 1, 0)
            value_part = product(prob_b, grad, 1, 0)
            key_grad = key_part if key_grad is None else key_grad + key_part
            value_grad = value_part if value_grad is None else value_grad + value_part
        for which, total in enumerate((key_grad, value_grad)):
            pieces = [total[d * rows : (d + 1) * rows] for d in range(REACH + 1)]
            gm_out[core, h, which] = pieces[1].astype(jnp.bfloat16)
            gm_out[1 - core, h, which] = pieces[3].astype(jnp.bfloat16)
            for place in range(3):
                gacc[place, h, which] = pieces[2 * place]

    for h in range(AHEAD):
        stage_other(h)
    stage_mate(0)

    def step(i, carry):
        @pl.when(i + AHEAD < HK)
        def _():
            stage_other(i + AHEAD)

        @pl.when(i + 1 < HK)
        def _():
            stage_mate(i + 1)

        @pl.when(i < HK)
        def _():
            remote(
                kv.at[2, i], kv.at[1 + 2 * core, i], m_send.at[0, i], m_recv.at[0, i], mate
            ).wait_recv()
            remote(
                kv.at[0, i], kv.at[3 - 2 * core, i], m_send.at[1, i], m_recv.at[1, i], mate
            ).wait_recv()
            attend(i)
            grad_mate(i, 0).start()
            grad_mate(i, 1).start()

        @pl.when((i >= 1) & (i < HK + 1))
        def _():
            h = i - 1
            grad_mate(h, 0).wait_recv()
            grad_mate(h, 1).wait_recv()
            gacc[1, h] += gm_in[0, h].astype(jnp.float32)
            gacc[2 * core, h] += gm_in[1, h].astype(jnp.float32)
            gx_out[h] = gacc[1, h].astype(jnp.bfloat16)
            grad_other(h).start()

        @pl.when((i >= 2) & (i < HK + 2))
        def _():
            h = i - 2
            grad_other(h).wait_recv()
            gacc[2 * x, h] += gx_in[h].astype(jnp.float32)

            @pl.when(has_before)
            def _():
                gz_out[h] = gacc[2, h].astype(jnp.bfloat16)
                grad_before(h).start()

        @pl.when(i >= 3)
        def _():
            h = i - 3

            @pl.when(has_after)
            def _():
                grad_before(h).wait_recv()
                gacc[0, h] += gz_in[h].astype(jnp.float32)

            columns = pl.ds(pl.multiple_of(h * HD, HD), HD)
            dk_ref[:, columns] = gacc[0, h, 0].astype(jnp.bfloat16)
            dv_ref[:, columns] = gacc[0, h, 1].astype(jnp.bfloat16)

        return carry

    lax.fori_loop(0, HK + 3, step, 0)

    def finish(h, carry):
        @pl.when(has_after)
        def _():
            to_after(h).wait_send()

        to_other(h).wait_send()
        to_mate_a(h).wait_send()
        to_mate_b(h).wait_send()
        grad_mate(h, 0).wait_send()
        grad_mate(h, 1).wait_send()
        grad_other(h).wait_send()

        @pl.when(has_before)
        def _():
            grad_before(h).wait_send()

        return carry

    lax.fori_loop(0, HK, finish, 0)


def per_device(quads, queries, keys, values, out_grad):
    rows = queries.shape[0]
    pair = (2, rows, HD)
    one = pltpu.SemaphoreType.DMA((HK,))
    two = pltpu.SemaphoreType.DMA((2, HK))
    vmem = pl.BlockSpec(memory_space=pltpu.VMEM)
    hbm = pl.BlockSpec(memory_space=pl.ANY)
    return pl.pallas_call(
        functools.partial(kernel, quads),
        out_shape=(
            jax.ShapeDtypeStruct(queries.shape, jnp.bfloat16),
            jax.ShapeDtypeStruct(queries.shape, jnp.bfloat16),
            jax.ShapeDtypeStruct(keys.shape, jnp.bfloat16),
            jax.ShapeDtypeStruct(keys.shape, jnp.bfloat16),
        ),
        in_specs=[vmem, vmem, hbm, hbm],
        out_specs=(vmem, vmem, vmem, vmem),
        scratch_shapes=[
            pltpu.VMEM((REACH + 1, HK) + pair, jnp.bfloat16),
            pltpu.VMEM((3, HK) + pair, jnp.float32),
            pltpu.VMEM((2, HK) + pair, jnp.bfloat16),
            pltpu.VMEM((2, HK) + pair, jnp.bfloat16),
            pltpu.VMEM((HK,) + pair, jnp.bfloat16),
            pltpu.VMEM((HK,) + pair, jnp.bfloat16),
            pltpu.VMEM((HK,) + pair, jnp.bfloat16),
            pltpu.VMEM((HK,) + pair, jnp.bfloat16),
            two,
            one,
            one,
            one,
            one,
            two,
            two,
            one,
            one,
            one,
            one,
            two,
            two,
        ],
        compiler_params=pltpu.CompilerParams(
            collective_id=0, has_side_effects=True, vmem_limit_bytes=60000 * 1024
        ),
    )(queries, out_grad, keys, values)


def solution(mesh):
    spec = P(("groups", "seq"), None)
    return jax.shard_map(
        functools.partial(per_device, mesh.shape["seq"] // 4),
        mesh=mesh,
        in_specs=(spec, spec, spec, spec),
        out_specs=(spec, spec, spec, spec),
        check_vma=False,
    )
```

```python
import functools

import jax
import jax.numpy as jnp
from jax import lax
from jax.experimental import pallas as pl
from jax.experimental.pallas import tpu as pltpu
from jax.sharding import PartitionSpec as P

HQ = 16
HK = 8
HD = 128
WINDOW = 1024
REACH = 4
LAG = 4

query_scale = 168.0 ** (-0.5)


def product(left, right, left_dim, right_dim):
    return lax.dot_general(
        left, right, (((left_dim,), (right_dim,)), ((), ())), preferred_element_type=jnp.float32
    )


def kernel(
    quads,
    q_hbm,
    g_hbm,
    k_hbm,
    v_hbm,
    att_ref,
    dq_ref,
    dk_ref,
    dv_ref,
    kv,
    gacc,
    gm_out,
    gm_in,
    gx_out,
    gx_in,
    gz_out,
    gz_in,
    part,
    q_ref,
    g_ref,
    own_sem,
    q_sem,
    z_send,
    z_recv,
    x_send,
    x_recv,
    m_send,
    m_recv,
    gz_send,
    gz_recv,
    gx_send,
    gx_recv,
    gm_send,
    gm_recv,
):
    rows = q_hbm.shape[0]
    me = lax.axis_index("seq")
    quad = me // 4
    x = (me // 2) % 2
    core = me % 2
    other = me + 2 - 4 * x
    mate = me + 1 - 2 * core
    has_before = quad > 0
    has_after = quad < quads - 1
    after = jnp.where(has_after, me + 4, me)
    before = jnp.where(has_before, me - 4, me)

    def remote(src, dst, send, recv, target):
        return pltpu.make_async_remote_copy(
            src_ref=src,
            dst_ref=dst,
            send_sem=send,
            recv_sem=recv,
            device_id={"seq": target},
            device_id_type=pl.DeviceIdType.MESH,
        )

    def own_copy(h, which):
        source = (k_hbm, v_hbm)[which]
        return pltpu.make_async_copy(
            source.at[:, pl.ds(pl.multiple_of(h * HD, HD), HD)],
            kv.at[0, h, which],
            own_sem.at[which, h],
        )

    def to_after(h):
        return remote(kv.at[0, h], kv.at[4, h], z_send.at[h], z_recv.at[h], after)

    def to_other(h):
        return remote(kv.at[4 * x, h], kv.at[2, h], x_send.at[h], x_recv.at[h], other)

    def to_mate_a(h):
        return remote(
            kv.at[2, h], kv.at[3 - 2 * core, h], m_send.at[0, h], m_recv.at[0, h], mate
        )

    def to_mate_b(h):
        return remote(
            kv.at[4 * core, h], kv.at[1 + 2 * core, h], m_send.at[1, h], m_recv.at[1, h], mate
        )

    def grad_mate(h, which):
        return remote(
            gm_out.at[which, h],
            gm_in.at[which, h],
            gm_send.at[which, h],
            gm_recv.at[which, h],
            mate,
        )

    def grad_other(h):
        return remote(gx_out.at[h], gx_in.at[h], gx_send.at[h], gx_recv.at[h], other)

    def grad_before(h):
        return remote(gz_out.at[h], gz_in.at[h], gz_send.at[h], gz_recv.at[h], before)

    for h in range(HK):
        own_copy(h, 0).start()
        own_copy(h, 1).start()
    query_copy = pltpu.make_async_copy(q_hbm, q_ref, q_sem.at[0])
    grad_copy = pltpu.make_async_copy(g_hbm, g_ref, q_sem.at[1])
    query_copy.start()
    grad_copy.start()

    barrier = pltpu.get_barrier_semaphore()
    for target in (other, mate):
        pl.semaphore_signal(
            barrier, inc=1, device_id={"seq": target}, device_id_type=pl.DeviceIdType.MESH
        )

    @pl.when(has_before)
    def _():
        pl.semaphore_signal(
            barrier, inc=1, device_id={"seq": before}, device_id_type=pl.DeviceIdType.MESH
        )

    @pl.when(has_after)
    def _():
        pl.semaphore_signal(
            barrier, inc=1, device_id={"seq": after}, device_id_type=pl.DeviceIdType.MESH
        )

    @pl.when(jnp.logical_not(has_before))
    def _():
        kv[4] = jnp.zeros(kv.shape[1:], kv.dtype)

    pl.semaphore_wait(
        barrier, 2 + jnp.where(has_before, 1, 0) + jnp.where(has_after, 1, 0)
    )

    def start_after(h, carry):
        own_copy(h, 0).wait()
        own_copy(h, 1).wait()

        @pl.when(has_after)
        def _():
            to_after(h).start()

        @pl.when(x == 0)
        def _():
            to_other(h).start()

        return carry

    lax.fori_loop(0, HK, start_after, 0)

    def stage_other(h):
        @pl.when(has_before)
        def _():
            to_after(h).wait_recv()

        @pl.when(x == 1)
        def _():
            to_other(h).start()

    def stage_mate(h):
        to_other(h).wait_recv()
        to_mate_a(h).start()
        to_mate_b(h).start()

    key_ids = lax.broadcasted_iota(jnp.int32, (rows, rows), 0)
    query_ids = lax.broadcasted_iota(jnp.int32, (rows, rows), 1)

    def attend(h, j, last):
        extent = (REACH + 1) * rows
        key_all = kv[:, h, 0].reshape(extent, HD)
        value_all = kv[:, h, 1].reshape(extent, HD)
        columns = pl.ds(pl.multiple_of(h * (HQ // HK * HD) + j * HD, HD), HD)
        query = q_ref[:, columns]
        grad = g_ref[:, columns]
        scores = product(key_all, query, 1, 1) * query_scale
        parts = [scores[d * rows : (d + 1) * rows] for d in range(REACH + 1)]
        parts[0] = jnp.where(key_ids <= query_ids, parts[0], jnp.float32(-1e30))
        parts[REACH] = jnp.where(key_ids > query_ids, parts[REACH], jnp.float32(-1e30))
        outside = [jnp.where(me >= d, jnp.float32(0), jnp.float32(1e30)) for d in range(REACH + 1)]
        peak = jnp.max(parts[0], axis=0, keepdims=True)
        for d in range(1, REACH + 1):
            peak = jnp.maximum(peak, jnp.max(parts[d], axis=0, keepdims=True) - outside[d])
        expo = jnp.concatenate(
            [jnp.exp(parts[d] - (peak + outside[d])) for d in range(REACH + 1)], axis=0
        )
        prob = expo * (1.0 / jnp.sum(expo, axis=0, keepdims=True))
        prob_b = prob.astype(jnp.bfloat16)
        attended = product(value_all, prob_b, 0, 0)
        att_ref[:, columns] = attended.T.astype(jnp.bfloat16)
        delta = jnp.sum(attended * grad.astype(jnp.float32).T, axis=0, keepdims=True)
        dprob = product(value_all, grad, 1, 1)
        dscore = (query_scale * prob * (dprob - delta)).astype(jnp.bfloat16)
        query_grad = product(key_all, dscore, 0, 0)
        dq_ref[:, columns] = query_grad.T.astype(jnp.bfloat16)
        for which, total in enumerate((product(dscore, query, 1, 0), product(prob_b, grad, 1, 0))):
            if not last:
                part[which] = total
                continue
            total = total + part[which]
            pieces = [total[d * rows : (d + 1) * rows] for d in range(REACH + 1)]
            gm_out[core, h, which] = pieces[1].astype(jnp.bfloat16)
            gm_out[1 - core, h, which] = pieces[3].astype(jnp.bfloat16)
            for place in range(3):
                gacc[place, h, which] = pieces[2 * place]

    def stage_grad_other(h):
        grad_mate(h, 0).wait_recv()
        grad_mate(h, 1).wait_recv()
        gacc[1, h] += gm_in[0, h].astype(jnp.float32)
        gacc[2 * core, h] += gm_in[1, h].astype(jnp.float32)
        gx_out[h] = gacc[1, h].astype(jnp.bfloat16)
        grad_other(h).start()

        @pl.when(has_before & (x == 0))
        def _():
            gz_out[h] = gacc[2, h].astype(jnp.bfloat16)
            grad_before(h).start()

    def stage_grad_before(h):
        grad_other(h).wait_recv()
        gacc[2 * x, h] += gx_in[h].astype(jnp.float32)

        @pl.when(has_before & (x == 1))
        def _():
            gz_out[h] = gacc[2, h].astype(jnp.bfloat16)
            grad_before(h).start()

    def stage_final(h):
        @pl.when(has_after)
        def _():
            grad_before(h).wait_recv()
            gacc[0, h] += gz_in[h].astype(jnp.float32)

        columns = pl.ds(pl.multiple_of(h * HD, HD), HD)
        dk_ref[:, columns] = gacc[0, h, 0].astype(jnp.bfloat16)
        dv_ref[:, columns] = gacc[0, h, 1].astype(jnp.bfloat16)

    stage_other(0)
    stage_other(1)
    stage_mate(0)
    query_copy.wait()
    grad_copy.wait()
    stage_other(2)

    def step(i, carry):
        @pl.when((i >= 1) & (2 * i + 2 < HK))
        def _():
            stage_other(2 * i + 2)

        remote(
            kv.at[2, i], kv.at[1 + 2 * core, i], m_send.at[0, i], m_recv.at[0, i], mate
        ).wait_recv()
        remote(
            kv.at[0, i], kv.at[3 - 2 * core, i], m_send.at[1, i], m_recv.at[1, i], mate
        ).wait_recv()
        attend(i, 0, False)

        @pl.when(2 * i + 3 < HK)
        def _():
            stage_other(2 * i + 3)

        @pl.when(i + 1 < HK)
        def _():
            stage_mate(i + 1)

        @pl.when(i >= 1)
        def _():
            stage_grad_other(i - 1)

        @pl.when(i >= LAG)
        def _():
            stage_grad_before(i - LAG)

        attend(i, 1, True)
        grad_mate(i, 0).start()
        grad_mate(i, 1).start()
        return carry

    lax.fori_loop(0, HK, step, 0)
    stage_grad_other(HK - 1)

    def drain(n, carry):
        stage_grad_before(n + HK - LAG)

        @pl.when(n < HK - LAG)
        def _():
            stage_final(n)

        return carry

    lax.fori_loop(0, LAG, drain, 0)

    def last_final(h, carry):
        stage_final(h)
        return carry

    lax.fori_loop(min(LAG, HK - LAG), HK, last_final, 0)

    def finish(h, carry):
        @pl.when(has_after)
        def _():
            to_after(h).wait_send()

        to_other(h).wait_send()
        to_mate_a(h).wait_send()
        to_mate_b(h).wait_send()
        grad_mate(h, 0).wait_send()
        grad_mate(h, 1).wait_send()
        grad_other(h).wait_send()

        @pl.when(has_before)
        def _():
            grad_before(h).wait_send()

        return carry

    lax.fori_loop(0, HK, finish, 0)


def per_device(quads, queries, keys, values, out_grad):
    rows = queries.shape[0]
    pair = (2, rows, HD)
    one = pltpu.SemaphoreType.DMA((HK,))
    two = pltpu.SemaphoreType.DMA((2, HK))
    vmem = pl.BlockSpec(memory_space=pltpu.VMEM)
    hbm = pl.BlockSpec(memory_space=pltpu.HBM)
    return pl.pallas_call(
        functools.partial(kernel, quads),
        out_shape=(
            jax.ShapeDtypeStruct(queries.shape, jnp.bfloat16),
            jax.ShapeDtypeStruct(queries.shape, jnp.bfloat16),
            jax.ShapeDtypeStruct(keys.shape, jnp.bfloat16),
            jax.ShapeDtypeStruct(keys.shape, jnp.bfloat16),
        ),
        in_specs=[hbm, hbm, hbm, hbm],
        out_specs=(vmem, vmem, vmem, vmem),
        scratch_shapes=[
            pltpu.VMEM((REACH + 1, HK) + pair, jnp.bfloat16),
            pltpu.VMEM((3, HK) + pair, jnp.float32),
            pltpu.VMEM((2, HK) + pair, jnp.bfloat16),
            pltpu.VMEM((2, HK) + pair, jnp.bfloat16),
            pltpu.VMEM((HK,) + pair, jnp.bfloat16),
            pltpu.VMEM((HK,) + pair, jnp.bfloat16),
            pltpu.VMEM((HK,) + pair, jnp.bfloat16),
            pltpu.VMEM((HK,) + pair, jnp.bfloat16),
            pltpu.VMEM((2, (REACH + 1) * rows, HD), jnp.float32),
            pltpu.VMEM(queries.shape, jnp.bfloat16),
            pltpu.VMEM(queries.shape, jnp.bfloat16),
            two,
            pltpu.SemaphoreType.DMA((2,)),
            one,
            one,
            one,
            one,
            two,
            two,
            one,
            one,
            one,
            one,
            two,
            two,
        ],
        compiler_params=pltpu.CompilerParams(
            collective_id=0, has_side_effects=True, vmem_limit_bytes=42000 * 1024
        ),
    )(
        *(
            pltpu.with_memory_space_constraint(array, pltpu.HBM)
            for array in (queries, out_grad, keys, values)
        )
    )


def solution(mesh):
    spec = P(("groups", "seq"), None)
    return jax.shard_map(
        functools.partial(per_device, mesh.shape["seq"] // 4),
        mesh=mesh,
        in_specs=(spec, spec, spec, spec),
        out_specs=(spec, spec, spec, spec),
        check_vma=False,
    )
```

```python
import functools

import jax
import jax.numpy as jnp
from jax import lax
from jax.experimental import pallas as pl
from jax.experimental.pallas import tpu as pltpu
from jax.sharding import PartitionSpec as P

HQ = 16
HK = 8
HD = 128
WINDOW = 1024
REACH = 4
LAG = 3

query_scale = 168.0 ** (-0.5)
exponent_scale = query_scale * 1.4426950408889634


def product(left, right, left_dim, right_dim):
    return lax.dot_general(
        left, right, (((left_dim,), (right_dim,)), ((), ())), preferred_element_type=jnp.float32
    )


def kernel(
    quads,
    q_hbm,
    g_hbm,
    k_hbm,
    v_hbm,
    att_ref,
    dq_ref,
    dk_ref,
    dv_ref,
    kv,
    gacc,
    gm_out,
    gm_in,
    gx_out,
    gx_in,
    gz_out,
    gz_in,
    part,
    q_ref,
    g_ref,
    own_sem,
    q_sem,
    z_send,
    z_recv,
    x_send,
    x_recv,
    m_send,
    m_recv,
    gz_send,
    gz_recv,
    gx_send,
    gx_recv,
    gm_send,
    gm_recv,
):
    rows = q_hbm.shape[0]
    me = lax.axis_index("seq")
    quad = me // 4
    x = (me // 2) % 2
    core = me % 2
    other = me + 2 - 4 * x
    mate = me + 1 - 2 * core
    has_before = quad > 0
    has_after = quad < quads - 1
    after = jnp.where(has_after, me + 4, me)
    before = jnp.where(has_before, me - 4, me)

    def remote(src, dst, send, recv, target):
        return pltpu.make_async_remote_copy(
            src_ref=src,
            dst_ref=dst,
            send_sem=send,
            recv_sem=recv,
            device_id={"seq": target},
            device_id_type=pl.DeviceIdType.MESH,
        )

    def own_copy(h, which):
        source = (k_hbm, v_hbm)[which]
        return pltpu.make_async_copy(
            source.at[:, pl.ds(pl.multiple_of(h * HD, HD), HD)],
            kv.at[0, h, which],
            own_sem.at[which, h],
        )

    def to_after(h):
        return remote(kv.at[0, h], kv.at[4, h], z_send.at[h], z_recv.at[h], after)

    def to_other(h):
        return remote(kv.at[4 * x, h], kv.at[2, h], x_send.at[h], x_recv.at[h], other)

    def to_mate_a(h):
        return remote(
            kv.at[2, h], kv.at[3 - 2 * core, h], m_send.at[0, h], m_recv.at[0, h], mate
        )

    def to_mate_b(h):
        return remote(
            kv.at[4 * core, h], kv.at[1 + 2 * core, h], m_send.at[1, h], m_recv.at[1, h], mate
        )

    def grad_mate(h, which):
        return remote(
            gm_out.at[which, h],
            gm_in.at[which, h],
            gm_send.at[which, h],
            gm_recv.at[which, h],
            mate,
        )

    def grad_other(h):
        return remote(gx_out.at[h], gx_in.at[h], gx_send.at[h], gx_recv.at[h], other)

    def grad_before(h):
        return remote(gz_out.at[h], gz_in.at[h], gz_send.at[h], gz_recv.at[h], before)

    for h in range(HK):
        own_copy(h, 0).start()
        own_copy(h, 1).start()
    query_copy = pltpu.make_async_copy(q_hbm, q_ref, q_sem.at[0])
    grad_copy = pltpu.make_async_copy(g_hbm, g_ref, q_sem.at[1])
    query_copy.start()
    grad_copy.start()

    barrier = pltpu.get_barrier_semaphore()
    for target in (other, mate):
        pl.semaphore_signal(
            barrier, inc=1, device_id={"seq": target}, device_id_type=pl.DeviceIdType.MESH
        )

    @pl.when(has_before)
    def _():
        pl.semaphore_signal(
            barrier, inc=1, device_id={"seq": before}, device_id_type=pl.DeviceIdType.MESH
        )

    @pl.when(has_after)
    def _():
        pl.semaphore_signal(
            barrier, inc=1, device_id={"seq": after}, device_id_type=pl.DeviceIdType.MESH
        )

    @pl.when(jnp.logical_not(has_before))
    def _():
        kv[4] = jnp.zeros(kv.shape[1:], kv.dtype)

    pl.semaphore_wait(
        barrier, 2 + jnp.where(has_before, 1, 0) + jnp.where(has_after, 1, 0)
    )

    def start_after(h, carry):
        own_copy(h, 0).wait()
        own_copy(h, 1).wait()

        @pl.when(has_after)
        def _():
            to_after(h).start()

        @pl.when(x == 0)
        def _():
            to_other(h).start()

        return carry

    lax.fori_loop(0, HK, start_after, 0)

    def stage_other(h):
        @pl.when(has_before)
        def _():
            to_after(h).wait_recv()

        @pl.when(x == 1)
        def _():
            to_other(h).start()

    def stage_mate(h):
        to_other(h).wait_recv()
        to_mate_a(h).start()
        to_mate_b(h).start()

    key_ids = lax.broadcasted_iota(jnp.int32, (rows, rows), 0)
    query_ids = lax.broadcasted_iota(jnp.int32, (rows, rows), 1)

    def attend(h, j, last):
        extent = (REACH + 1) * rows
        key_all = kv[:, h, 0].reshape(extent, HD)
        value_all = kv[:, h, 1].reshape(extent, HD)
        columns = pl.ds(pl.multiple_of(h * (HQ // HK * HD) + j * HD, HD), HD)
        query = q_ref[:, columns]
        grad = g_ref[:, columns]
        scores = product(key_all, query, 1, 1)
        parts = [scores[d * rows : (d + 1) * rows] for d in range(REACH + 1)]
        parts[0] = jnp.where(key_ids <= query_ids, parts[0], jnp.float32(-1e30))
        parts[REACH] = jnp.where(key_ids > query_ids, parts[REACH], jnp.float32(-1e30))
        outside = [jnp.where(me >= d, jnp.float32(0), jnp.float32(1e30)) for d in range(REACH + 1)]
        peak = jnp.max(parts[0], axis=0, keepdims=True)
        for d in range(1, REACH + 1):
            peak = jnp.maximum(peak, jnp.max(parts[d], axis=0, keepdims=True) - outside[d])
        expo = jnp.concatenate(
            [
                jnp.exp2((parts[d] - (peak + outside[d])) * exponent_scale)
                for d in range(REACH + 1)
            ],
            axis=0,
        )
        prob = expo * (1.0 / jnp.sum(expo, axis=0, keepdims=True))
        prob_b = prob.astype(jnp.bfloat16)
        attended = product(value_all, prob_b, 0, 0)
        att_ref[:, columns] = attended.T.astype(jnp.bfloat16)
        delta = jnp.sum(attended * grad.astype(jnp.float32).T, axis=0, keepdims=True)
        dprob = product(value_all, grad, 1, 1)
        dscore = (query_scale * prob * (dprob - delta)).astype(jnp.bfloat16)
        query_grad = product(key_all, dscore, 0, 0)
        dq_ref[:, columns] = query_grad.T.astype(jnp.bfloat16)
        for which, total in enumerate((product(dscore, query, 1, 0), product(prob_b, grad, 1, 0))):
            if not last:
                part[which] = total
                continue
            total = total + part[which]
            pieces = [total[d * rows : (d + 1) * rows] for d in range(REACH + 1)]
            gm_out[core, h, which] = pieces[1].astype(jnp.bfloat16)
            gm_out[1 - core, h, which] = pieces[3].astype(jnp.bfloat16)
            for place in range(3):
                gacc[place, h, which] = pieces[2 * place]

    def stage_grad_other(h):
        grad_mate(h, 0).wait_recv()
        grad_mate(h, 1).wait_recv()
        gacc[1, h] += gm_in[0, h].astype(jnp.float32)
        gacc[2 * core, h] += gm_in[1, h].astype(jnp.float32)
        gx_out[h] = gacc[1, h].astype(jnp.bfloat16)
        grad_other(h).start()

        @pl.when(has_before & (x == 0))
        def _():
            gz_out[h] = gacc[2, h].astype(jnp.bfloat16)
            grad_before(h).start()

    def stage_grad_before(h):
        grad_other(h).wait_recv()
        gacc[2 * x, h] += gx_in[h].astype(jnp.float32)

        @pl.when(has_before & (x == 1))
        def _():
            gz_out[h] = gacc[2, h].astype(jnp.bfloat16)
            grad_before(h).start()

    def stage_final(h):
        @pl.when(has_after)
        def _():
            grad_before(h).wait_recv()
            gacc[0, h] += gz_in[h].astype(jnp.float32)

        columns = pl.ds(pl.multiple_of(h * HD, HD), HD)
        dk_ref[:, columns] = gacc[0, h, 0].astype(jnp.bfloat16)
        dv_ref[:, columns] = gacc[0, h, 1].astype(jnp.bfloat16)

    stage_other(0)
    stage_other(1)
    stage_mate(0)
    query_copy.wait()
    grad_copy.wait()
    stage_other(2)

    def step(i, carry):
        @pl.when((i >= 1) & (2 * i + 2 < HK))
        def _():
            stage_other(2 * i + 2)

        remote(
            kv.at[2, i], kv.at[1 + 2 * core, i], m_send.at[0, i], m_recv.at[0, i], mate
        ).wait_recv()
        remote(
            kv.at[0, i], kv.at[3 - 2 * core, i], m_send.at[1, i], m_recv.at[1, i], mate
        ).wait_recv()
        attend(i, 0, False)

        @pl.when(2 * i + 3 < HK)
        def _():
            stage_other(2 * i + 3)

        @pl.when(i + 1 < HK)
        def _():
            stage_mate(i + 1)

        @pl.when(i >= 1)
        def _():
            stage_grad_other(i - 1)

        @pl.when(i >= LAG)
        def _():
            stage_grad_before(i - LAG)

        attend(i, 1, True)
        grad_mate(i, 0).start()
        grad_mate(i, 1).start()
        return carry

    lax.fori_loop(0, HK, step, 0)
    stage_grad_other(HK - 1)

    def drain(n, carry):
        stage_grad_before(n + HK - LAG)

        @pl.when(n < HK - LAG)
        def _():
            stage_final(n)

        return carry

    lax.fori_loop(0, LAG, drain, 0)

    def last_final(h, carry):
        stage_final(h)
        return carry

    lax.fori_loop(min(LAG, HK - LAG), HK, last_final, 0)

    def finish(h, carry):
        @pl.when(has_after)
        def _():
            to_after(h).wait_send()

        to_other(h).wait_send()
        to_mate_a(h).wait_send()
        to_mate_b(h).wait_send()
        grad_mate(h, 0).wait_send()
        grad_mate(h, 1).wait_send()
        grad_other(h).wait_send()

        @pl.when(has_before)
        def _():
            grad_before(h).wait_send()

        return carry

    lax.fori_loop(0, HK, finish, 0)


def per_device(quads, queries, keys, values, out_grad):
    rows = queries.shape[0]
    pair = (2, rows, HD)
    one = pltpu.SemaphoreType.DMA((HK,))
    two = pltpu.SemaphoreType.DMA((2, HK))
    vmem = pl.BlockSpec(memory_space=pltpu.VMEM)
    hbm = pl.BlockSpec(memory_space=pltpu.HBM)
    return pl.pallas_call(
        functools.partial(kernel, quads),
        out_shape=(
            jax.ShapeDtypeStruct(queries.shape, jnp.bfloat16),
            jax.ShapeDtypeStruct(queries.shape, jnp.bfloat16),
            jax.ShapeDtypeStruct(keys.shape, jnp.bfloat16),
            jax.ShapeDtypeStruct(keys.shape, jnp.bfloat16),
        ),
        in_specs=[hbm, hbm, hbm, hbm],
        out_specs=(vmem, vmem, vmem, vmem),
        scratch_shapes=[
            pltpu.VMEM((REACH + 1, HK) + pair, jnp.bfloat16),
            pltpu.VMEM((3, HK) + pair, jnp.float32),
            pltpu.VMEM((2, HK) + pair, jnp.bfloat16),
            pltpu.VMEM((2, HK) + pair, jnp.bfloat16),
            pltpu.VMEM((HK,) + pair, jnp.bfloat16),
            pltpu.VMEM((HK,) + pair, jnp.bfloat16),
            pltpu.VMEM((HK,) + pair, jnp.bfloat16),
            pltpu.VMEM((HK,) + pair, jnp.bfloat16),
            pltpu.VMEM((2, (REACH + 1) * rows, HD), jnp.float32),
            pltpu.VMEM(queries.shape, jnp.bfloat16),
            pltpu.VMEM(queries.shape, jnp.bfloat16),
            two,
            pltpu.SemaphoreType.DMA((2,)),
            one,
            one,
            one,
            one,
            two,
            two,
            one,
            one,
            one,
            one,
            two,
            two,
        ],
        compiler_params=pltpu.CompilerParams(
            collective_id=0, has_side_effects=True, vmem_limit_bytes=42000 * 1024
        ),
    )(
        *(
            pltpu.with_memory_space_constraint(array, pltpu.HBM)
            for array in (queries, out_grad, keys, values)
        )
    )


def solution(mesh):
    spec = P(("groups", "seq"), None)
    return jax.shard_map(
        functools.partial(per_device, mesh.shape["seq"] // 4),
        mesh=mesh,
        in_specs=(spec, spec, spec, spec),
        out_specs=(spec, spec, spec, spec),
        check_vma=False,
    )
```
